32 devices in a mesh: lat: 4 (over y, x), lon: 8 (over z, core).
Axes of the slice: x: 2, y: 2, z: 4, core: 2. Of those that a mesh axis runs over, the one named last changes fastest.
Arguments:
- field: bfloat16 [4, 70, 128, 256], P(None, None, 'lat', 'lon'), may hold values from -6 to 6
- embed_weight: bfloat16 [1536, 1120], P(('lat', 'lon')), may hold values from -0.1875 to 0.1875
- embed_bias: float32 [1536], replicated, may hold values from -3 to 3
- embed_gain: float32 [1536], replicated, may hold values from 0.1 to 1.9
- embed_shift: float32 [1536], replicated, may hold values from -2 to 2
- qkv_weight: bfloat16 [1536, 2304], P(('lat', 'lon')), may hold values from -0.15625 to 0.15625
- logit_scale: float32 [12], replicated, may hold values from 1.6 to 5
- bias_table: float32 [12, 15, 15], replicated, may hold values from -6 to 6
- proj_weight: bfloat16 [1536, 768], P(('lat', 'lon')), may hold values from -0.21875 to 0.21875
- post_gain: float32 [1536], replicated, may hold values from 0.1 to 1.9
- post_shift: float32 [1536], replicated, may hold values from -2 to 2
Outputs:
- block_out: bfloat16 [4, 32, 64, 1536], P(None, 'lat', 'lon')
The draws below stay inside these ranges and needn't reach their ends.
All inputs are finite; a program needn't handle non-finite values.
Results may differ from the reference program's by a relative error of at most 0.011.
Values may be sent and summed in bfloat16 or wider, within the bound.
A program may use at most 128 MiB of HBM per device.

```python
import math
import jax
import jax.numpy as jnp
from jax import lax

VARS = 70
PATCH = 4
D = 1536
HEADS = 12
HD = 64
WIN = 8
BATCH = 4
INNER = 768
NLAT = 32
NLON = 64


def steps_of(own_key, dims, cuts, low, top_value):
    loudness, own = 1.0, jax.random.fold_in(own_key, 6)
    for dim, blocks in cuts:
        steps = jnp.exp(jax.random.uniform(jax.random.fold_in(own, dim), (blocks,), jnp.float32, low / len(cuts), top_value / len(cuts)))
        loudness = loudness * jnp.repeat(steps, dims[dim] // blocks).reshape([-1 if axis == dim else 1 for axis in range(len(dims))])
    return loudness


def gaussian(stream_key, dims, scale, reach, pieces=(), kind=jnp.bfloat16):
    array = jax.random.normal(stream_key, dims, jnp.float32) * scale
    if len(pieces) > 0:
        array = steps_of(stream_key, dims, pieces, -0.22, 0.18) * array
    return jnp.clip(array, min=-reach, max=reach).astype(kind)


def setup_inputs(seed: int = 0) -> dict:
    keys = jax.random.split(jax.random.key(seed), 12)
    field = gaussian(keys[0], (BATCH, VARS, NLAT * PATCH, NLON * PATCH), 1.0, 6.0, ((2, 4), (3, 8)))
    embed_weight = gaussian(keys[1], (D, VARS * PATCH * PATCH), (VARS * PATCH * PATCH) ** -0.5, 0.1875, ((0, 32),))
    embed_bias = gaussian(keys[2], (D,), 0.5, 3.0, (), jnp.float32)
    embed_gain = jnp.clip(1.0 + 0.18 * jax.random.normal(keys[3], (D,), jnp.float32), 0.1, 1.9)
    embed_shift = gaussian(keys[4], (D,), 0.3, 2.0, (), jnp.float32)
    qkv_weight = gaussian(keys[5], (D, 3 * INNER), D ** -0.5, 0.15625, ((0, 32),))
    logit_scale = jnp.clip(jax.random.uniform(keys[6], (HEADS,), jnp.float32, 1.6, 5.0), 1.6, 5.0)
    bias_table = gaussian(keys[7], (HEADS, 2 * WIN - 1, 2 * WIN - 1), 1.5, 6.0, (), jnp.float32)
    proj_weight = gaussian(keys[8], (D, INNER), INNER ** -0.5, 0.21875, ((0, 32),))
    post_gain = jnp.clip(1.0 + 0.18 * jax.random.normal(keys[9], (D,), jnp.float32), 0.1, 1.9)
    post_shift = gaussian(keys[10], (D,), 0.3, 2.0, (), jnp.float32)
    return {"field": field, "embed_weight": embed_weight, "embed_bias": embed_bias, "embed_gain": embed_gain, "embed_shift": embed_shift, "qkv_weight": qkv_weight, "logit_scale": logit_scale, "bias_table": bias_table, "proj_weight": proj_weight, "post_gain": post_gain, "post_shift": post_shift}


scale_cap = math.log(100.0)

def layer_norm(inputs, gain, shift):
    average = lax.optimization_barrier(jnp.mean(inputs, axis=-1, keepdims=True))
    centred = inputs - average
    spread = lax.optimization_barrier(jnp.mean(centred * centred, axis=-1, keepdims=True))
    return centred * lax.rsqrt(spread + 1e-05) * gain + shift

def window_bias(bias_table, window):
    places = jnp.arange(window * window, dtype=jnp.int32)
    row_place = places // window
    col_place = places % window
    row_gap = row_place[:, None] - row_place[None, :] + window - 1
    col_gap = col_place[:, None] - col_place[None, :] + window - 1
    table = 16.0 * jax.nn.sigmoid(bias_table)
    return table[:, row_gap, col_gap]

def cosine_unit(inputs):
    widened = inputs.astype(jnp.float32)
    total = lax.optimization_barrier(jnp.sum(widened * widened, axis=-1, keepdims=True))
    return (widened * lax.rsqrt(total + 1e-06)).astype(jnp.bfloat16)

def to_windows(grid_block, window):
    row_count, col_count, features = grid_block.shape
    shaped = grid_block.reshape(row_count // window, window, col_count // window, window, features)
    return shaped.transpose(0, 2, 1, 3, 4).reshape(-1, window * window, features)

def from_windows(windowed, row_count, col_count, window):
    features = windowed.shape[-1]
    shaped = windowed.reshape(row_count // window, col_count // window, window, window, features)
    return shaped.transpose(0, 2, 1, 3, 4).reshape(row_count, col_count, features)

def attend(qkv_block, row_groups, scales, bias):
    row_count, col_count = (qkv_block.shape[0], qkv_block.shape[1])
    inner = HEADS * HD
    windowed = to_windows(qkv_block, WIN).reshape(-1, WIN * WIN, 3, HEADS, HD)
    groups = jnp.broadcast_to(row_groups.reshape(row_count // WIN, 1, WIN, 1), (row_count // WIN, col_count // WIN, WIN, WIN)).reshape(-1, WIN * WIN)
    q_unit = cosine_unit(windowed[:, :, 0])
    k_unit = cosine_unit(windowed[:, :, 1])
    scores = jnp.einsum('wqhd,wkhd->whqk', q_unit.astype(jnp.float32), k_unit.astype(jnp.float32))
    scores = scores * scales[None, :, None, None] + bias[None]
    allowed = groups[:, :, None] == groups[:, None, :]
    scores = jnp.where(allowed[:, None], scores, jnp.float32(-1e+30))
    highest = lax.optimization_barrier(jnp.max(scores, axis=-1, keepdims=True))
    expo = jnp.exp(scores - highest)
    weights = (expo / lax.optimization_barrier(jnp.sum(expo, axis=-1, keepdims=True))).astype(jnp.bfloat16)
    attended = jnp.einsum('whqk,wkhd->wqhd', weights.astype(jnp.float32), windowed[:, :, 2].astype(jnp.float32))
    attended = attended.astype(jnp.bfloat16).reshape(-1, WIN * WIN, inner)
    return from_windows(attended, row_count, col_count, WIN)

def reference(field, embed_weight, embed_bias, embed_gain, embed_shift, qkv_weight, logit_scale, bias_table, proj_weight, post_gain, post_shift):
    lat_total = field.shape[2] // PATCH
    lon_total = field.shape[3] // PATCH
    patch_len = VARS * PATCH * PATCH
    offset = WIN // 2
    inner = HEADS * HD
    scales = jnp.exp(jnp.minimum(logit_scale, scale_cap))
    bias = window_bias(bias_table, WIN)
    band_count = lat_total // WIN

    def one_sample(sample):

        def embed_band(band_index):
            start = (band_index * WIN * PATCH).astype(jnp.int32)
            strip = lax.dynamic_slice_in_dim(sample, start, WIN * PATCH, 1)
            patches = strip.reshape(VARS, WIN, PATCH, lon_total, PATCH).transpose(1, 3, 0, 2, 4).reshape(WIN * lon_total, patch_len)
            embed_pre = jnp.dot(patches, embed_weight.T, preferred_element_type=jnp.float32) + embed_bias
            return layer_norm(embed_pre, embed_gain, embed_shift).astype(jnp.bfloat16).reshape(WIN, lon_total, D)
        tokens = lax.map(embed_band, jnp.arange(band_count, dtype=jnp.int32)).reshape(lat_total, lon_total, D)
        rolled = jnp.roll(tokens, (-offset, -offset), (0, 1))

        def block_band(band_index):
            start = (band_index * WIN).astype(jnp.int32)
            strip = lax.dynamic_slice_in_dim(rolled, start, WIN, 0)
            flat = strip.reshape(-1, D)
            qkv = jnp.dot(flat, qkv_weight, preferred_element_type=jnp.float32).astype(jnp.bfloat16)
            qkv = qkv.reshape(WIN, lon_total, 3 * inner)
            rolled_rows = start + jnp.arange(WIN, dtype=jnp.int32)
            global_rows = (rolled_rows + offset) % lat_total
            row_groups = jnp.where(global_rows < offset, -1, (global_rows - offset) // WIN).astype(jnp.int32)
            attended = attend(qkv, row_groups, scales, bias)
            projected = jnp.dot(attended.reshape(-1, inner), proj_weight.T, preferred_element_type=jnp.float32)
            mixed = flat.astype(jnp.float32) + layer_norm(projected, post_gain, post_shift)
            return mixed.astype(jnp.bfloat16).reshape(WIN, lon_total, D)
        result = lax.map(block_band, jnp.arange(band_count, dtype=jnp.int32)).reshape(lat_total, lon_total, D)
        return jnp.roll(result, (offset, offset), (0, 1))
    return lax.map(one_sample, field)
```

```python
import functools
import math

import jax
import jax.numpy as jnp
from jax import lax
from jax.experimental import pallas as pl
from jax.experimental.pallas import tpu as pltpu
from jax.sharding import PartitionSpec as P

VARS = 70
PATCH = 4
D = 1536
HEADS = 12
HD = 64
WIN = 8
HALF = WIN // 2
QUADS = 4
INNER = HEADS * HD

MESH = pl.DeviceIdType.MESH
VMEM_BYTES = 56 * 1024 * 1024

scale_cap = math.log(100.0)


def layer_norm(inputs, gain, shift):
    average = jnp.mean(inputs, axis=-1, keepdims=True)
    centred = inputs - average
    spread = jnp.mean(centred * centred, axis=-1, keepdims=True)
    return centred * lax.rsqrt(spread + 1e-05) * gain + shift


def dot_rows(left, right):
    return lax.dot_general(
        left, right, (((1,), (1,)), ((), ())), preferred_element_type=jnp.float32
    )


def dot_plain(left, right):
    return lax.dot_general(
        left, right, (((1,), (0,)), ((), ())), preferred_element_type=jnp.float32
    )


def iota(shape, dim):
    return lax.broadcasted_iota(jnp.int32, shape, dim)


def onehot(condition):
    return jnp.where(condition, 1.0, 0.0).astype(jnp.bfloat16)


def window_bias(bias_table):
    places = jnp.arange(WIN * WIN, dtype=jnp.int32)
    quad, rest = places // 16, places % 16
    row_place = quad // 2 * HALF + rest // HALF
    col_place = quad % 2 * HALF + rest % HALF
    row_gap = row_place[:, None] - row_place[None, :] + WIN - 1
    col_gap = col_place[:, None] - col_place[None, :] + WIN - 1
    levels = jnp.arange(2 * WIN - 1, dtype=jnp.int32)
    row_onehot = (row_gap[:, :, None] == levels).astype(jnp.float32)
    col_onehot = (col_gap[:, :, None] == levels).astype(jnp.float32)
    table = 16.0 * jax.nn.sigmoid(bias_table)
    by_rows = jnp.einsum("hrc,qkc->hqkr", table, col_onehot, precision=lax.Precision.HIGHEST)
    return jnp.sum(by_rows * row_onehot[None], axis=-1)


def patch_kernel(field_ref, out_ref, spread):
    batch = field_ref.shape[0]
    spread[...] = jnp.zeros_like(spread)
    side = WIN * PATCH
    pick_row = iota((side, side), 0)
    pick_col = iota((side, side), 1)
    pick = onehot(pick_col == (pick_row % WIN) * PATCH + pick_row // WIN)
    for sample in range(batch):
        for row in range(side):
            i, p = row // PATCH, row % PATCH
            picked = dot_rows(pick, field_ref[sample, row])
            for q in range(PATCH):
                lane = (p * PATCH + q) * 128
                spread[pl.ds((sample * WIN + i) * WIN, WIN), lane : lane + VARS] = picked[
                    q * WIN : (q + 1) * WIN
                ]
    tokens = batch * WIN * WIN
    to = iota((tokens, tokens), 0)
    source = iota((tokens, tokens), 1)
    per_quad = batch * 16
    quad, sample, place = to // per_quad, to % per_quad // 16, to % 16
    row = quad // 2 * HALF + place // HALF
    col = quad % 2 * HALF + place % HALF
    order = onehot(source == (sample * WIN + row) * WIN + col)
    length = VARS * PATCH * PATCH
    feature = iota((128, length), 1)
    same = feature // 16 == iota((128, length), 0)
    slot = feature % 16
    total = jnp.zeros((tokens, length), jnp.float32)
    for pq in range(16):
        piece = spread[:, pq * 128 : (pq + 1) * 128].astype(jnp.bfloat16)
        total = total + dot_plain(piece, onehot(same & (slot == pq)))
    out = dot_plain(order, total.astype(jnp.bfloat16)).astype(jnp.bfloat16)
    out_ref[...] = out.reshape(out_ref.shape)


def exchange_kernel(lat_size, lon_size, weights, patch_ref, *refs):
    local, outs = refs[:weights], refs[weights + 1 : 2 * weights + 1]
    rolled = refs[weights]
    send_sem, recv_sem, own_sem = refs[2 * weights + 1 :]
    lat, lon = lax.axis_index("lat"), lax.axis_index("lon")
    before = (lax.rem(lat + lat_size - 1, lat_size), lax.rem(lon + lon_size - 1, lon_size))
    after = (lax.rem(lat + 1, lat_size), lax.rem(lon + 1, lon_size))
    targets = [(lat, before[1]), (before[0], lon), (before[0], before[1])]
    sources = [(lat, after[1]), (after[0], lon), (after[0], after[1])]
    y, x = lat // 2, lax.rem(lat, 2)
    z, core = lon // 2, lax.rem(lon, 2)
    peers = []
    if weights:
        depth = lon_size // 2
        lat_x = y * 2 + 1 - x
        lat_y = (1 - y) * 2 + x
        lat_d = (1 - y) * 2 + 1 - x
        other = z * 2 + 1 - core

        def lon_at(k):
            return lax.rem(z + depth - k, depth) * 2 + core

        to_x, to_y, to_c = (lat_x, lon), (lat_y, lon), (lat, other)
        to_z = [(lat, lax.rem(z + k, depth) * 2 + core) for k in range(depth)]
        peers = [to_x, to_y, to_c] + to_z[1:]
    barrier = pltpu.get_barrier_semaphore()
    greeted = targets + sources + peers
    for peer in greeted:
        pl.semaphore_signal(barrier, inc=1, device_id=peer, device_id_type=MESH)
    pl.semaphore_wait(barrier, len(greeted))

    count = [0]
    started = []

    def send(src, dst, landing, device):
        index = count[0]
        count[0] += 1
        copy = pltpu.make_async_remote_copy(
            src_ref=src, dst_ref=dst, send_sem=send_sem.at[index], recv_sem=recv_sem.at[index],
            device_id=device, device_id_type=MESH,
        )
        copy.start()
        started.append(copy)
        return pltpu.make_async_remote_copy(
            src_ref=src, dst_ref=landing, send_sem=send_sem.at[index], recv_sem=recv_sem.at[index],
            device_id=device, device_id_type=MESH,
        )

    arrivals = []
    for slot in (1, 2, 3):
        arrivals.append(
            send(patch_ref.at[3 - slot], rolled.at[slot], rolled.at[slot], targets[slot - 1])
        )
    keeps = [pltpu.make_async_copy(patch_ref.at[3], rolled.at[0], own_sem.at[0])]
    if weights:
        me = lat * lon_size + lon
        for t in range(weights):
            keeps.append(pltpu.make_async_copy(local[t], outs[t].at[me], own_sem.at[t + 1]))
    for keep in keeps:
        keep.start()
    if weights:

        def at(row, k, own=True):
            return row * lon_size + (lon_at(k) if own else lax.rem(z + depth - k, depth) * 2 + 1 - core)

        z_in, x_in, y_in = {}, {}, {}

        def fan(t, k, src):
            dst = outs[t].at[at(lat, k)]
            x_in[t, k] = send(src, dst, outs[t].at[at(lat_x, k)], to_x)
            y_in[t, k] = send(src, dst, outs[t].at[at(lat_y, k)], to_y)
            arrivals.append(send(src, dst, outs[t].at[at(lat, k, False)], to_c))

        for t in range(weights):
            for k in range(1, depth):
                z_in[t, k] = send(local[t], outs[t].at[me], outs[t].at[at(lat, k)], to_z[k])
            fan(t, 0, local[t])
        for t in range(weights):
            rows = local[t].shape[0]
            d_in = {}
            for k in range(1, depth):
                z_in[t, k].wait_recv()
                fan(t, k, outs[t].at[at(lat, k)])
            for k in range(depth):
                cut = rows // 3 // 16 * 16 * (1 + k % 2)
                x_in[t, k].wait_recv()
                block = outs[t].at[at(lat_x, k)]
                first = block.at[0:cut]
                d_one = send(first, first, outs[t].at[at(lat_d, k)].at[0:cut], to_y)
                arrivals.append(send(block, block, outs[t].at[at(lat_x, k, False)], to_c))
                y_in[t, k].wait_recv()
                block = outs[t].at[at(lat_y, k)]
                second = block.at[cut:rows]
                d_two = send(second, second, outs[t].at[at(lat_d, k)].at[cut:rows], to_x)
                arrivals.append(send(block, block, outs[t].at[at(lat_y, k, False)], to_c))
                d_in[k] = (d_one, d_two)
            for k in range(depth):
                for half in d_in[k]:
                    half.wait_recv()
                block = outs[t].at[at(lat_d, k)]
                arrivals.append(send(block, block, outs[t].at[at(lat_d, k, False)], to_c))
    for keep in keeps:
        keep.wait()
    for copy in arrivals:
        copy.wait_recv()
    for copy in started:
        copy.wait_send()


def exchange(mesh_shape, patches, tensors):
    lat_size, lon_size = mesh_shape
    weights = len(tensors)
    devices = lat_size * lon_size
    depth = lon_size // 2
    copies = 3 + weights * (depth - 1 + 2 * depth + 2 * depth + 4 * depth)
    anywhere = pl.BlockSpec(memory_space=pl.ANY)
    return pl.pallas_call(
        functools.partial(exchange_kernel, lat_size, lon_size, weights),
        out_shape=[jax.ShapeDtypeStruct(patches.shape, patches.dtype)]
        + [jax.ShapeDtypeStruct((devices,) + t.shape, t.dtype) for t in tensors],
        in_specs=[anywhere] * (1 + weights),
        out_specs=[anywhere] * (1 + weights),
        scratch_shapes=[
            pltpu.SemaphoreType.DMA((copies,)),
            pltpu.SemaphoreType.DMA((copies,)),
            pltpu.SemaphoreType.DMA((1 + weights,)),
        ],
        compiler_params=pltpu.CompilerParams(collective_id=0, has_side_effects=True),
    )(patches, *tensors)


def return_kernel(lat_size, lon_size, source_ref, out_ref, send_sem, recv_sem, own_sem):
    lat, lon = lax.axis_index("lat"), lax.axis_index("lon")
    before = (lax.rem(lat + lat_size - 1, lat_size), lax.rem(lon + lon_size - 1, lon_size))
    after = (lax.rem(lat + 1, lat_size), lax.rem(lon + 1, lon_size))
    sources = [(lat, before[1]), (before[0], lon), (before[0], before[1])]
    targets = [(lat, after[1]), (after[0], lon), (after[0], after[1])]
    barrier = pltpu.get_barrier_semaphore()
    for peer in targets + sources:
        pl.semaphore_signal(barrier, inc=1, device_id=peer, device_id_type=MESH)
    keep = pltpu.make_async_copy(source_ref.at[0], out_ref.at[3], own_sem)
    keep.start()
    pl.semaphore_wait(barrier, 6)
    copies = []
    for slot in (1, 2, 3):
        copies.append(
            pltpu.make_async_remote_copy(
                src_ref=source_ref.at[slot], dst_ref=out_ref.at[3 - slot],
                send_sem=send_sem.at[slot - 1], recv_sem=recv_sem.at[slot - 1],
                device_id=targets[slot - 1], device_id_type=MESH,
            )
        )
        copies[-1].start()
    keep.wait()
    for copy in copies:
        copy.wait()


def give_back(mesh_shape, attended):
    whole = pl.BlockSpec(memory_space=pltpu.VMEM)
    return pl.pallas_call(
        functools.partial(return_kernel, *mesh_shape),
        out_shape=jax.ShapeDtypeStruct(attended.shape, attended.dtype),
        in_specs=[whole],
        out_specs=whole,
        scratch_shapes=[
            pltpu.SemaphoreType.DMA((3,)),
            pltpu.SemaphoreType.DMA((3,)),
            pltpu.SemaphoreType.DMA,
        ],
        compiler_params=pltpu.CompilerParams(collective_id=1, has_side_effects=True),
    )(attended)


def unit(inputs):
    total = jnp.sum(inputs * inputs, axis=-1, keepdims=True)
    return (inputs * lax.rsqrt(total + 1e-06)).astype(jnp.bfloat16)


def block_kernel(
    lat_size, rolled_ref, local_ref, embed_ref, ebias_ref, egain_ref, eshift_ref, qkv_ref,
    scale_ref, bias_ref, attended_ref, tokens_ref,
):
    quads, rows, length = rolled_ref.shape
    count = quads * rows
    last = lax.axis_index("lat") == lat_size - 1

    def embed(ref):
        pre = dot_rows(ref[...].reshape(count, length), embed_ref[...]) + ebias_ref[...]
        return layer_norm(pre, egain_ref[...], eshift_ref[...]).astype(jnp.bfloat16)

    tokens = embed(rolled_ref)
    qkv = dot_plain(tokens, qkv_ref[...]).astype(jnp.bfloat16)
    tokens_ref[...] = embed(local_ref).reshape(tokens_ref.shape)
    batch = rows // 16
    qkv = qkv.reshape(quads, batch, 16, 3 * INNER)
    qkv = jnp.concatenate(
        [qkv[quad, sample] for sample in range(batch) for quad in range(quads)], axis=0
    )
    window = WIN * WIN
    one, two = iota((count, count), 0), iota((count, count), 1)
    apart = jnp.where(last, 1, 0) * jnp.abs((one % window) // 32 - (two % window) // 32)
    allowed = (one // window == two // window) & (apart == 0)
    for head in range(HEADS):
        lanes = head * HD
        query = unit(qkv[:, lanes : lanes + HD].astype(jnp.float32))
        key = unit(qkv[:, INNER + lanes : INNER + lanes + HD].astype(jnp.float32))
        value = qkv[:, 2 * INNER + lanes : 2 * INNER + lanes + HD]
        table = bias_ref[head]
        table = jnp.concatenate([table] * batch, axis=1)
        table = jnp.concatenate([table] * batch, axis=0)
        scores = dot_rows(query, key) * scale_ref[head] + table
        scores = jnp.where(allowed, scores, -1e30)
        expo = jnp.exp(scores - jnp.max(scores, axis=-1, keepdims=True))
        attn = (expo / jnp.sum(expo, axis=-1, keepdims=True)).astype(jnp.bfloat16)
        attended = dot_plain(attn, value).astype(jnp.bfloat16)
        for sample in range(batch):
            for quad in range(quads):
                start = sample * window + quad * 16
                attended_ref[quad, sample * 16 : sample * 16 + 16, lanes : lanes + HD] = attended[
                    start : start + 16
                ]


def final_kernel(attended_ref, tokens_ref, proj_ref, gain_ref, shift_ref, out_ref):
    quads, rows, inner = attended_ref.shape
    batch = rows // 16
    projected = dot_rows(attended_ref[...].reshape(quads * rows, inner), proj_ref[...])
    normed = layer_norm(projected, gain_ref[...], shift_ref[...])
    mixed = tokens_ref[...].reshape(quads * rows, D).astype(jnp.float32) + normed
    for quad in range(quads):
        for sample in range(batch):
            for r in range(HALF):
                start = quad * rows + sample * 16 + r * HALF
                col = quad % 2 * HALF
                out_ref[sample, quad // 2 * HALF + r, col : col + HALF, :] = mixed[
                    start : start + HALF
                ].astype(jnp.bfloat16)


def on_device(
    mesh_shape, field, embed_weight, embed_bias, embed_gain, embed_shift, qkv_weight,
    logit_scale, bias_table, proj_weight, post_gain, post_shift,
):
    batch = field.shape[0]
    per_quad = batch * 16
    length = VARS * PATCH * PATCH
    whole = pl.BlockSpec(memory_space=pltpu.VMEM)
    params = pltpu.CompilerParams(vmem_limit_bytes=VMEM_BYTES)
    scales = jnp.exp(jnp.minimum(logit_scale, scale_cap))
    bias = window_bias(bias_table)
    patches = pl.pallas_call(
        patch_kernel,
        out_shape=jax.ShapeDtypeStruct((QUADS, per_quad, length), jnp.bfloat16),
        in_specs=[whole],
        out_specs=whole,
        scratch_shapes=[pltpu.VMEM((batch * WIN * WIN, 16 * 128), jnp.float32)],
        compiler_params=params,
    )(field.transpose(0, 2, 1, 3))
    if mesh_shape == (4, 8):
        rolled, embed_all, qkv_all, proj_all = exchange(
            mesh_shape, patches, (embed_weight, qkv_weight, proj_weight)
        )
        embed_all = embed_all.reshape(D, -1)
        qkv_all = qkv_all.reshape(D, -1)
        proj_all = proj_all.reshape(D, -1)
    else:
        (rolled,) = exchange(mesh_shape, patches, ())
        embed_all, qkv_all, proj_all = (
            lax.all_gather(
                lax.all_gather(weight, "lon", axis=0, tiled=True), "lat", axis=0, tiled=True
            )
            for weight in (embed_weight, qkv_weight, proj_weight)
        )
    attended, tokens = pl.pallas_call(
        functools.partial(block_kernel, mesh_shape[0]),
        out_shape=[
            jax.ShapeDtypeStruct((QUADS, per_quad, INNER), jnp.bfloat16),
            jax.ShapeDtypeStruct((QUADS, per_quad, D), jnp.bfloat16),
        ],
        in_specs=[whole] * 7 + [pl.BlockSpec(memory_space=pltpu.SMEM), whole],
        out_specs=[whole] * 2,
        compiler_params=params,
    )(
        rolled, patches, embed_all, embed_bias.reshape(1, -1), embed_gain.reshape(1, -1),
        embed_shift.reshape(1, -1), qkv_all, scales, bias,
    )
    attended = give_back(mesh_shape, attended)
    return pl.pallas_call(
        final_kernel,
        out_shape=jax.ShapeDtypeStruct((batch, WIN, WIN, D), jnp.bfloat16),
        in_specs=[whole] * 5,
        out_specs=whole,
        compiler_params=params,
    )(attended, tokens, proj_all, post_gain.reshape(1, -1), post_shift.reshape(1, -1))


def solution(mesh):
    placed = (
        P(None, None, "lat", "lon"),
        P(("lat", "lon"), None),
        P(),
        P(),
        P(),
        P(("lat", "lon"), None),
        P(),
        P(),
        P(("lat", "lon"), None),
        P(),
        P(),
    )
    return jax.shard_map(
        functools.partial(on_device, (mesh.shape["lat"], mesh.shape["lon"])),
        mesh=mesh,
        in_specs=placed,
        out_specs=P(None, "lat", "lon", None),
        check_vma=False,
    )
```

```python
import functools
import math

import jax
import jax.numpy as jnp
from jax import lax
from jax.experimental import pallas as pl
from jax.experimental.pallas import tpu as pltpu
from jax.sharding import PartitionSpec as P

VARS = 70
PATCH = 4
D = 1536
HEADS = 12
HD = 64
WIN = 8
HALF = WIN // 2
QUADS = 4
INNER = HEADS * HD

MESH = pl.DeviceIdType.MESH
VMEM_BYTES = 56 * 1024 * 1024

scale_cap = math.log(100.0)


def layer_norm(inputs, gain, shift):
    average = jnp.mean(inputs, axis=-1, keepdims=True)
    centred = inputs - average
    spread = jnp.mean(centred * centred, axis=-1, keepdims=True)
    return centred * lax.rsqrt(spread + 1e-05) * gain + shift


def dot_rows(left, right):
    return lax.dot_general(
        left, right, (((1,), (1,)), ((), ())), preferred_element_type=jnp.float32
    )


def dot_plain(left, right):
    return lax.dot_general(
        left, right, (((1,), (0,)), ((), ())), preferred_element_type=jnp.float32
    )


def iota(shape, dim):
    return lax.broadcasted_iota(jnp.int32, shape, dim)


def onehot(condition):
    return jnp.where(condition, 1.0, 0.0).astype(jnp.bfloat16)


def bias_into(table_ref, padded, bias):
    heads = table_ref.shape[0]
    span = 2 * WIN - 1
    padded[...] = jnp.zeros_like(padded)
    for level in range(span):
        padded[0:heads, level * 16 : level * 16 + span] = table_ref[:, level, :]
    table = 16.0 * jax.nn.sigmoid(padded[...])
    high = table.astype(jnp.bfloat16)
    rest = table - high.astype(jnp.float32)
    middle = rest.astype(jnp.bfloat16)
    low = (rest - middle.astype(jnp.float32)).astype(jnp.bfloat16)
    parts = jnp.concatenate([high, middle, low], axis=0)
    places = WIN * WIN
    entry = iota((256, places), 0)
    key = iota((256, places), 1)
    key_row = key // 32 * HALF + key % 16 // HALF
    key_col = key // 16 % 2 * HALF + key % HALF
    for query in range(places):
        row = query // 32 * HALF + query % 16 // HALF
        col = query // 16 % 2 * HALF + query % HALF
        wanted = (row + WIN - 1 - key_row) * 16 + (col + WIN - 1 - key_col)
        found = dot_plain(parts, onehot(entry == wanted))
        bias[query] = found[0:16] + found[16:32] + found[32:48]


def patch_into(field_ref, spread, out):
    batch = field_ref.shape[0]
    spread[...] = jnp.zeros_like(spread)
    side = WIN * PATCH
    pick_row = iota((side, side), 0)
    pick_col = iota((side, side), 1)
    pick = onehot(pick_col == (pick_row % WIN) * PATCH + pick_row // WIN)
    for sample in range(batch):
        for row in range(side):
            i, p = row // PATCH, row % PATCH
            picked = dot_plain(pick, field_ref[sample, row])
            for q in range(PATCH):
                lane = (p * PATCH + q) * 128
                spread[pl.ds((sample * WIN + i) * WIN, WIN), lane : lane + VARS] = picked[
                    q * WIN : (q + 1) * WIN
                ]
    tokens = batch * WIN * WIN
    to = iota((tokens, tokens), 0)
    source = iota((tokens, tokens), 1)
    per_quad = batch * 16
    quad, sample, place = to // per_quad, to % per_quad // 16, to % 16
    row = quad // 2 * HALF + place // HALF
    col = quad % 2 * HALF + place % HALF
    order = onehot(source == (sample * WIN + row) * WIN + col)
    length = VARS * PATCH * PATCH
    feature = iota((128, length), 1)
    same = feature // 16 == iota((128, length), 0)
    slot = feature % 16
    total = jnp.zeros((tokens, length), jnp.float32)
    for pq in range(16):
        piece = spread[:, pq * 128 : (pq + 1) * 128].astype(jnp.bfloat16)
        total = total + dot_plain(piece, onehot(same & (slot == pq)))
    out[...] = dot_plain(order, total.astype(jnp.bfloat16)).astype(jnp.bfloat16).reshape(out.shape)


def unit(inputs):
    total = jnp.sum(inputs * inputs, axis=-1, keepdims=True)
    return (inputs * lax.rsqrt(total + 1e-06)).astype(jnp.bfloat16)


E, Q, J = 0, 1, 2

STEPS = (
    "patch X00 Y00 Z01".split() + "X10 Y10 Z02 X20".split() + "Y20 Z03 X01 Y01".split()
    + "bias X02 Y02 Z11".split() + "X03 Y03 Z12".split() + "D00 D01 D02 D03".split()
    + "local X11 Y11 rolled".split() + "Z13 X12 Y12 Z21".split() + "Z22 Z23 X13 Y13".split()
    + "D10 X21 Y21 D11".split() + "X22 Y22 D12 X23".split() + "Y23 D13 qkv attend".split()
    + "D20 D21 D22 D23".split() + "final".split()
)


def whole_kernel(
    lat_size, lon_size, gather, field_ref, embed_ref, qkv_ref, proj_ref, ebias_ref, egain_ref,
    eshift_ref, scale_ref, table_ref, pgain_ref, pshift_ref, out_ref, embed_all, qkv_all,
    proj_all, spread, patches, rolled, tokens, moved, qkv, attended, returned, padded, bias,
    send_sem, recv_sem, own_sem,
):
    local, outs = (embed_ref, qkv_ref, proj_ref), (embed_all, qkv_all, proj_all)
    lat, lon = lax.axis_index("lat"), lax.axis_index("lon")
    before = (lax.rem(lat + lat_size - 1, lat_size), lax.rem(lon + lon_size - 1, lon_size))
    after = (lax.rem(lat + 1, lat_size), lax.rem(lon + 1, lon_size))
    backward = [(lat, before[1]), (before[0], lon), (before[0], before[1])]
    forward = [(lat, after[1]), (after[0], lon), (after[0], after[1])]
    y, x = lat // 2, lax.rem(lat, 2)
    z, core = lon // 2, lax.rem(lon, 2)
    greeted = backward + forward
    depth = lon_size // 2
    if gather:
        lat_x = y * 2 + 1 - x
        lat_y = (1 - y) * 2 + x
        lat_d = (1 - y) * 2 + 1 - x
        to_x, to_y, to_c = (lat_x, lon), (lat_y, lon), (lat, z * 2 + 1 - core)
        to_z = [(lat, lax.rem(z + k, depth) * 2 + core) for k in range(depth)]
        greeted = greeted + [to_x, to_y, to_c] + to_z[1:]
    barrier = pltpu.get_barrier_semaphore()
    for peer in greeted:
        pl.semaphore_signal(barrier, inc=1, device_id=peer, device_id_type=MESH)
    me = lat * lon_size + lon
    keeps = []
    for t in (E, Q, J):
        keep = outs[t].at[me] if gather else outs[t]
        keeps.append(pltpu.make_async_copy(local[t], keep, own_sem.at[t]))
    for keep in keeps:
        keep.start()
    pl.semaphore_wait(barrier, len(greeted))

    count = [0]
    started = []

    def send(src, dst, landing, device):
        index = count[0]
        count[0] += 1

        def copy(to):
            return pltpu.make_async_remote_copy(
                src_ref=src, dst_ref=to, send_sem=send_sem.at[index],
                recv_sem=recv_sem.at[index], device_id=device, device_id_type=MESH,
            )

        going = copy(dst)
        going.start()
        started.append(going)
        return copy(landing)

    def at(row, k, sibling=False):
        side = 1 - core if sibling else core
        return row * lon_size + lax.rem(z + depth - k, depth) * 2 + side

    z_in, x_in, y_in, d_in, c_in = {}, {}, {}, {}, {E: [], Q: [], J: []}

    def across(t, row, k, src):
        dst = outs[t].at[at(row, k)]
        c_in[t].append(send(src, dst, outs[t].at[at(row, k, True)], to_c))

    def fan(t, k, src):
        dst = outs[t].at[at(lat, k)]
        x_in[t, k] = send(src, dst, outs[t].at[at(lat_x, k)], to_x)
        y_in[t, k] = send(src, dst, outs[t].at[at(lat_y, k)], to_y)
        across(t, lat, k, src)

    def pass_on(kind, t, k):
        rows = outs[t].shape[1]
        cut = rows // 3 // 16 * 16 * (1 + k % 2)
        far = outs[t].at[at(lat_d, k)]
        if kind == "Z":
            z_in[t, k].wait_recv()
            fan(t, k, outs[t].at[at(lat, k)])
        elif kind == "X":
            x_in[t, k].wait_recv()
            block = outs[t].at[at(lat_x, k)]
            part = block.at[0:cut]
            d_in[t, k, 0] = send(part, part, far.at[0:cut], to_y)
            across(t, lat_x, k, block)
        elif kind == "Y":
            y_in[t, k].wait_recv()
            block = outs[t].at[at(lat_y, k)]
            part = block.at[cut:rows]
            d_in[t, k, 1] = send(part, part, far.at[cut:rows], to_x)
            across(t, lat_y, k, block)
        else:
            d_in[t, k, 0].wait_recv()
            d_in[t, k, 1].wait_recv()
            across(t, lat_d, k, far)

    def have(t):
        keeps[t].wait()
        for copy in c_in[t]:
            copy.wait_recv()

    if gather:
        for t in (E, Q, J):
            for k in range(1, depth):
                z_in[t, k] = send(local[t], outs[t].at[me], outs[t].at[at(lat, k)], to_z[k])
            fan(t, 0, local[t])

    quads, rows, length = patches.shape
    batch = rows // 16
    window = WIN * WIN
    total = quads * rows
    halo = []

    def embed(ref, into):
        weight = embed_all[...].reshape(D, length)
        pre = dot_rows(ref[...].reshape(total, length), weight) + ebias_ref[...].reshape(1, D)
        gain, shift = egain_ref[...].reshape(1, D), eshift_ref[...].reshape(1, D)
        into[...] = layer_norm(pre, gain, shift).astype(jnp.bfloat16)

    def attend():
        last = lat == lat_size - 1
        one, two = iota((total, total), 0), iota((total, total), 1)
        apart = jnp.where(last, 1, 0) * jnp.abs((one % window) // 32 - (two % window) // 32)
        allowed = (one // window == two // window) & (apart == 0)
        for head in range(HEADS):
            lanes = head * HD
            query = unit(qkv[:, lanes : lanes + HD].astype(jnp.float32))
            key = unit(qkv[:, INNER + lanes : INNER + lanes + HD].astype(jnp.float32))
            value = qkv[:, 2 * INNER + lanes : 2 * INNER + lanes + HD]
            near = bias[:, head, :]
            near = jnp.concatenate([near] * batch, axis=1)
            near = jnp.concatenate([near] * batch, axis=0)
            scale = jnp.exp(jnp.minimum(jnp.full((1, total), scale_ref[head]), scale_cap))
            scores = dot_rows(query, key) * scale + near
            scores = jnp.where(allowed, scores, -1e30)
            expo = jnp.exp(scores - jnp.max(scores, axis=-1, keepdims=True))
            attn = (expo / jnp.sum(expo, axis=-1, keepdims=True)).astype(jnp.bfloat16)
            result = dot_plain(attn, value).astype(jnp.bfloat16)
            for sample in range(batch):
                for quad in range(quads):
                    start = sample * window + quad * 16
                    attended[quad, sample * 16 : sample * 16 + 16, lanes : lanes + HD] = result[
                        start : start + 16
                    ]

    backs = []
    for step in STEPS:
        if step == "patch":
            patch_into(field_ref, spread, patches)
            for slot in (1, 2, 3):
                halo.append(
                    send(patches.at[3 - slot], rolled.at[slot], rolled.at[slot], backward[slot - 1])
                )
            rolled[0] = patches[3]
        elif step == "bias":
            bias_into(table_ref, padded, bias)
        elif step == "local":
            have(E)
            embed(patches, tokens)
        elif step == "rolled":
            for copy in halo:
                copy.wait_recv()
            embed(rolled, moved)
        elif step == "qkv":
            have(Q)
            part = dot_plain(moved[...], qkv_all[...].reshape(D, 3 * INNER)).astype(jnp.bfloat16)
            for quad in range(quads):
                for sample in range(batch):
                    start = quad * rows + sample * 16
                    to = sample * window + quad * 16
                    qkv[to : to + 16, :] = part[start : start + 16]
        elif step == "attend":
            attend()
            for slot in (1, 2, 3):
                landing = returned.at[3 - slot]
                backs.append(send(attended.at[slot], landing, landing, forward[slot - 1]))
            returned[3] = attended[0]
        elif step == "final":
            have(J)
            for copy in backs:
                copy.wait_recv()
            weight = proj_all[...].reshape(D, INNER)
            projected = dot_rows(returned[...].reshape(total, INNER), weight)
            gain, shift = pgain_ref[...].reshape(1, D), pshift_ref[...].reshape(1, D)
            mixed = tokens[...].astype(jnp.float32) + layer_norm(projected, gain, shift)
            for quad in range(quads):
                for sample in range(batch):
                    for r in range(HALF):
                        start = quad * rows + sample * 16 + r * HALF
                        col = quad % 2 * HALF
                        out_ref[sample, quad // 2 * HALF + r, col : col + HALF, :] = mixed[
                            start : start + HALF
                        ].astype(jnp.bfloat16)
        elif gather:
            pass_on(step[0], int(step[1]), int(step[2]))
    for copy in started:
        copy.wait_send()


def on_device(
    mesh_shape, field, embed_weight, embed_bias, embed_gain, embed_shift, qkv_weight,
    logit_scale, bias_table, proj_weight, post_gain, post_shift,
):
    batch = field.shape[0]
    per_quad = batch * 16
    total = QUADS * per_quad
    length = VARS * PATCH * PATCH
    whole = pl.BlockSpec(memory_space=pltpu.VMEM)
    anywhere = pl.BlockSpec(memory_space=pl.ANY)
    weights = (embed_weight, qkv_weight, proj_weight)
    gather = mesh_shape == (4, 8)
    devices = mesh_shape[0] * mesh_shape[1]
    if gather:
        blocks = [(devices,) + weight.shape for weight in weights]
    else:
        weights = [
            lax.all_gather(
                lax.all_gather(weight, "lon", axis=0, tiled=True), "lat", axis=0, tiled=True
            )
            for weight in weights
        ]
        blocks = [weight.shape for weight in weights]
    copies = 6 + (3 * 35 if gather else 0)
    bf16, f32 = jnp.bfloat16, jnp.float32
    return pl.pallas_call(
        functools.partial(whole_kernel, mesh_shape[0], mesh_shape[1], gather),
        out_shape=jax.ShapeDtypeStruct((batch, WIN, WIN, D), bf16),
        in_specs=[whole] + [anywhere] * 3 + [whole] * 3
        + [pl.BlockSpec(memory_space=pltpu.SMEM)] + [whole] * 3,
        out_specs=whole,
        scratch_shapes=[pltpu.VMEM(shape, bf16) for shape in blocks]
        + [
            pltpu.VMEM((total, 16 * 128), f32),
            pltpu.VMEM((QUADS, per_quad, length), bf16),
            pltpu.VMEM((QUADS, per_quad, length), bf16),
            pltpu.VMEM((total, D), bf16),
            pltpu.VMEM((total, D), bf16),
            pltpu.VMEM((total, 3 * INNER), bf16),
            pltpu.VMEM((QUADS, per_quad, INNER), bf16),
            pltpu.VMEM((QUADS, per_quad, INNER), bf16),
            pltpu.VMEM((16, 256), f32),
            pltpu.VMEM((WIN * WIN, 16, WIN * WIN), f32),
            pltpu.SemaphoreType.DMA((copies,)),
            pltpu.SemaphoreType.DMA((copies,)),
            pltpu.SemaphoreType.DMA((3,)),
        ],
        compiler_params=pltpu.CompilerParams(
            collective_id=0, has_side_effects=True, vmem_limit_bytes=VMEM_BYTES
        ),
    )(
        field.transpose(0, 2, 3, 1), *weights, embed_bias, embed_gain, embed_shift, logit_scale,
        bias_table, post_gain, post_shift,
    )


def solution(mesh):
    placed = (
        P(None, None, "lat", "lon"),
        P(("lat", "lon"), None),
        P(),
        P(),
        P(),
        P(("lat", "lon"), None),
        P(),
        P(),
        P(("lat", "lon"), None),
        P(),
        P(),
    )
    return jax.shard_map(
        functools.partial(on_device, (mesh.shape["lat"], mesh.shape["lon"])),
        mesh=mesh,
        in_specs=placed,
        out_specs=P(None, "lat", "lon", None),
        check_vma=False,
    )
```
